32 devices in a mesh: tok: 2 (over y), lat: 16 (over z, x, core).
Axes of the slice: x: 2, y: 2, z: 4, core: 2. Of those that a mesh axis runs over, the one named last changes fastest.
Arguments:
- tokens: bfloat16 [512, 8192], P(('tok', 'lat')), may hold values from -6 to 6
- enc_weight: bfloat16 [8192, 4096], P(None, 'lat'), may hold values from -0.0625 to 0.0625
- enc_bias: float32 [4096], P('lat'), may hold values from -3 to 3
- dec_weight: bfloat16 [4096, 8192], P('lat'), may hold values from -0.125 to 0.125
- dec_bias: float32 [8192], replicated, may hold values from -3 to 3
- active_blocks: int32 [4, 8], P('tok'), may hold values from 0 to 15, all different within a row
Outputs:
- reconstruction: bfloat16 [512, 8192], P(('tok', 'lat'))
- enc_grad: float32 [8192, 4096], P('tok', 'lat')
- dec_grad: float32 [4096, 8192], P('lat', 'tok')
The draws below stay inside these ranges and needn't reach their ends.
Inputs may be any that keep to these rules, and one draw needn't show every extreme that they name: `active_blocks`: each row lists 8 different latent blocks, and every latent block is listed by some row.
All inputs are finite; a program needn't handle non-finite values.
Results may differ from the reference program's by a relative error of at most 0.013.
Values may be sent and summed in bfloat16 or wider, within the bound.
A program may use at most 64 MiB of HBM per device.

```python
import math
import jax
import jax.numpy as jnp
from jax import lax

D = 8192
LB = 256
BLK = 128
BLK_DEV = 1
SLOTS = 8
GB = 2
NB = 16
LATENTS = 4096
TOKEN_BLOCKS = 4
TOKENS = 512
GROUP = 256
N_LAT = 16


def block_scale(stream_key, extent, cuts, least, top_value):
    def one(axis_at, blocks):
        steps = jax.random.uniform(jax.random.fold_in(jax.random.fold_in(stream_key, 6), axis_at), (blocks,), jnp.float32, least / len(cuts), top_value / len(cuts))
        return jnp.repeat(jnp.exp(steps), extent[axis_at] // blocks).reshape((-1,) + (1,) * (len(extent) - axis_at - 1))

    level = one(*cuts[0])
    for cut in cuts[1:]:
        level = level * one(*cut)
    return level


def choose_distinct(stream_key, rows, count, top, lift):
    order = jax.random.permutation(jax.random.fold_in(stream_key, 1), count)
    pull = order
    for power in range(3):
        pull = pull * pull // count
    pull = pull * lift // count
    tickets = jax.random.randint(jax.random.fold_in(stream_key, 2), (rows, count), 0, 4096) + pull
    fixed_rows = jax.random.permutation(jax.random.fold_in(stream_key, 3), rows)[jnp.arange(count) % rows]
    tickets = jnp.where(jnp.arange(rows)[:, None] == fixed_rows[None, :], 1 << 14, tickets)
    priority = tickets * count + jnp.arange(count)
    return lax.top_k(priority.astype(jnp.int32), top)[1].astype(jnp.int32)


def noise(key, shape, scale, limit, cuts=(), kind=jnp.bfloat16):
    gain = block_scale(key, shape, cuts, -0.22, 0.18) if cuts else 1.0
    entries = jax.random.normal(key, shape, jnp.float32) * scale * gain
    return jnp.minimum(jnp.maximum(entries, -limit), limit).astype(kind)


def setup_inputs(seed: int = 0) -> dict:
    streams_of = jax.random.split(jax.random.key(seed), 7)
    tokens = noise(streams_of[0], (TOKENS, D), 1.0, 6.0, ((0, 32),))
    enc_weight = noise(streams_of[1], (D, LATENTS), D ** -0.5, 0.0625, ((1, 16),))
    enc_bias = noise(streams_of[2], (LATENTS,), 0.5, 3.0, ((0, 16),), jnp.float32)
    dec_weight = noise(streams_of[3], (LATENTS, D), (SLOTS * LB) ** -0.5, 0.125, ((0, 16),))
    dec_bias = noise(streams_of[4], (D,), 0.5, 3.0, (), jnp.float32)
    active_blocks = choose_distinct(streams_of[5], TOKEN_BLOCKS, NB, SLOTS, 8192)
    return dict(tokens=tokens, enc_weight=enc_weight, enc_bias=enc_bias, dec_weight=dec_weight, dec_bias=dec_bias, active_blocks=active_blocks)


def reference(tokens, enc_weight, enc_bias, dec_weight, dec_bias, active_blocks):
    latent_width = BLK_DEV * LB
    block_ids = jnp.arange(NB, dtype=jnp.int32)
    block_hits = jnp.any(active_blocks[:, :, None] == block_ids[None, None, :], axis=1).astype(jnp.float32)
    latent_gate = jnp.repeat(jnp.repeat(block_hits, LB, axis=1), BLK, axis=0)
    pre_act = jnp.dot(tokens, enc_weight, preferred_element_type=jnp.float32) + enc_bias.astype(jnp.float32)[None, :]
    activations = (jax.nn.silu(pre_act) * latent_gate).astype(jnp.bfloat16)

    def owner_term(running, owner_index):
        first_col = (owner_index * latent_width).astype(jnp.int32)
        owner_acts = lax.dynamic_slice_in_dim(activations, first_col, latent_width, 1)
        owner_rows = lax.dynamic_slice_in_dim(dec_weight, first_col, latent_width, 0)
        owner_part = jnp.dot(owner_acts, owner_rows, preferred_element_type=jnp.float32)
        owner_part = lax.optimization_barrier(owner_part.astype(jnp.bfloat16))
        return (running + owner_part.astype(jnp.float32), None)
    summed, _ = lax.scan(owner_term, jnp.zeros((TOKENS, D), jnp.float32), jnp.arange(N_LAT, dtype=jnp.int32))
    decoded = summed + dec_bias.astype(jnp.float32)[None, :]
    reconstruction = decoded.astype(jnp.bfloat16)
    cotangent = ((decoded - tokens.astype(jnp.float32)) * (1.0 / math.sqrt(TOKENS))).astype(jnp.bfloat16)
    latent_grad = jnp.dot(cotangent, dec_weight.T, preferred_element_type=jnp.float32)
    sigma = jax.nn.sigmoid(pre_act)
    pre_grad = (latent_grad * (sigma * (1.0 + pre_act * (1.0 - sigma))) * latent_gate).astype(jnp.bfloat16)

    def group_term(totals, group_index):
        enc_total, dec_total = totals
        first_row = (group_index * GROUP).astype(jnp.int32)
        group_tokens = lax.dynamic_slice_in_dim(tokens, first_row, GROUP, 0)
        group_grad = lax.dynamic_slice_in_dim(pre_grad, first_row, GROUP, 0)
        group_acts = lax.dynamic_slice_in_dim(activations, first_row, GROUP, 0)
        group_cot = lax.dynamic_slice_in_dim(cotangent, first_row, GROUP, 0)
        enc_part = jnp.dot(group_tokens.T, group_grad, preferred_element_type=jnp.float32)
        enc_part = lax.optimization_barrier(enc_part.astype(jnp.bfloat16))
        dec_part = jnp.dot(group_acts.T, group_cot, preferred_element_type=jnp.float32)
        dec_part = lax.optimization_barrier(dec_part.astype(jnp.bfloat16))
        return ((enc_total + enc_part.astype(jnp.float32), dec_total + dec_part.astype(jnp.float32)), None)
    start_totals = (jnp.zeros((D, LATENTS), jnp.float32), jnp.zeros((LATENTS, D), jnp.float32))
    totals, _ = lax.scan(group_term, start_totals, jnp.arange(TOKEN_BLOCKS // GB, dtype=jnp.int32))
    return (reconstruction, totals[0], totals[1])
```

```python
import functools
import math

import jax
import jax.numpy as jnp
from jax import lax
from jax.experimental import pallas as pl
from jax.experimental.pallas import tpu as pltpu
from jax.sharding import PartitionSpec as P

LB = 256
MESH = pl.DeviceIdType.MESH
NZ, NX, NC = 4, 2, 2
Z_ORDER = (2, 1, 3)
BF16 = jnp.bfloat16
F32 = jnp.float32


def contract_rows(left_rows, right_rows):
    return lax.dot_general(
        left_rows, right_rows, (((0,), (0,)), ((), ())), preferred_element_type=jnp.float32
    )


def fused_kernel(
    cot_scale,
    tok_hbm, encw_hbm, encb_ref, decw_hbm, decb_ref, blocks_ref,
    recon_ref, toks_out, cots_out, acts_out, grads_out,
    encw, decw, G, O, C, CO, PT, CR, XS, XR, ZS, ZR, pre, act, act_o, pg, pg_o,
    local_sem, g_send, g_recv, o_recv, c_send, c_recv, co_recv,
    r_send, cr_recv, xr_recv, zr_recv, small_send, small_recv,
):
    t = lax.axis_index("tok")
    l = lax.axis_index("lat")
    z, x, c = l // (NX * NC), (l // NC) % NX, l % NC
    rows, width = tok_hbm.shape
    half = width // 2

    def lat_of(dz, dx, dc):
        zz = lax.rem(z + dz, NZ)
        xx = x if dx == 0 else 1 - x
        cc = c if dc == 0 else 1 - c
        return (zz * NX + xx) * NC + cc

    own = lat_of(0, 0, 0)
    z_peer = {dz: (t, lat_of(dz, 0, 0)) for dz in Z_ORDER}
    x_peer = (t, lat_of(0, 1, 0))
    c_peer = (t, lat_of(0, 0, 1))
    y_peer = (1 - t, l)

    local = [
        pltpu.make_async_copy(tok_hbm, G.at[own], local_sem.at[0]),
        pltpu.make_async_copy(encw_hbm, encw, local_sem.at[1]),
        pltpu.make_async_copy(decw_hbm, decw, local_sem.at[2]),
    ]
    for copy in local:
        copy.start()

    barrier = pltpu.get_barrier_semaphore()
    peers = [z_peer[dz] for dz in Z_ORDER] + [x_peer, c_peer, y_peer]
    for peer in peers:
        pl.semaphore_signal(barrier, inc=1, device_id=peer, device_id_type=MESH)
    pl.semaphore_wait(barrier, len(peers))

    sent = []

    def push(src, dst, send_sem, recv_sem, peer):
        copy = pltpu.make_async_remote_copy(
            src_ref=src, dst_ref=dst, send_sem=send_sem, recv_sem=recv_sem,
            device_id=peer, device_id_type=MESH,
        )
        copy.start()
        sent.append(copy)

    def arrived(dst, send_sem, recv_sem):
        pltpu.make_async_remote_copy(
            src_ref=dst, dst_ref=dst, send_sem=send_sem, recv_sem=recv_sem,
            device_id=c_peer, device_id_type=MESH,
        ).wait_recv()

    mine = pl.ds(pl.multiple_of(t * half, half), half)
    theirs = pl.ds(pl.multiple_of((1 - t) * half, half), half)

    class Gather:
        def __init__(self, full, other, send, recv, other_recv):
            self.full, self.other = full, other
            self.send, self.recv, self.other_recv = send, recv, other_recv
            self.count = 0

        def next_send(self):
            self.count += 1
            return self.send.at[self.count - 1]

        def give(self, s, peer):
            push(self.full.at[s], self.full.at[s], self.next_send(), self.recv.at[s], peer)

        def give_y(self, s):
            push(
                self.full.at[s, :, theirs], self.other.at[s], self.next_send(),
                self.other_recv.at[s], y_peer,
            )

        def take(self, s):
            arrived(self.full.at[s], self.send.at[0], self.recv.at[s])

        def spread(self):
            for dz in Z_ORDER:
                self.give(own, z_peer[dz])
            self.give(own, x_peer)
            self.give_y(own)
            self.give(own, c_peer)

            def from_z(dz):
                s = lat_of(dz, 0, 0)
                self.take(s)
                self.give(s, x_peer)
                self.give_y(s)
                self.give(s, c_peer)

            def from_x(dz):
                s = lat_of(dz, 1, 0)
                self.take(s)
                self.give_y(s)
                self.give(s, c_peer)

            from_z(Z_ORDER[0])
            from_x(0)
            for at in range(1, 3):
                from_z(Z_ORDER[at])
                from_x(Z_ORDER[at - 1])
            from_x(Z_ORDER[2])

        def relay_other(self):
            for dx in range(NX):
                for dz in (0,) + Z_ORDER:
                    s = lat_of(dz, dx, 0)
                    arrived(self.other.at[s], self.send.at[0], self.other_recv.at[s])
                    push(
                        self.other.at[s], self.other.at[s], self.next_send(),
                        self.other_recv.at[s], c_peer,
                    )

        def settle(self):
            for dx in range(NX):
                for dz in (0,) + Z_ORDER:
                    self.take(lat_of(dz, dx, 1))

        def settle_other(self):
            for dx in range(NX):
                for dz in (0,) + Z_ORDER:
                    s = lat_of(dz, dx, 1)
                    arrived(self.other.at[s], self.send.at[0], self.other_recv.at[s])

    local[0].wait()
    toks = Gather(G, O, g_send, g_recv, o_recv)
    toks.spread()
    toks.settle()

    group_rows = G.shape[0] * rows
    lat_width = encw.shape[1]
    local[1].wait()
    tile = 1024
    pre[...] = jnp.broadcast_to(encb_ref[...], pre.shape)

    @pl.loop(0, width // tile)
    def _(k):
        cols = pl.ds(pl.multiple_of(k * tile, tile), tile)
        pre[...] += jnp.dot(
            G[:, :, cols].reshape(group_rows, tile), encw[cols, :], preferred_element_type=F32
        )

    block_count = blocks_ref.shape[0]
    block_rows = group_rows // block_count
    gates = []
    for b in range(block_count):
        hit = blocks_ref[b, 0] == l
        for slot in range(1, blocks_ref.shape[1]):
            hit = jnp.logical_or(hit, blocks_ref[b, slot] == l)
        gates.append(jnp.where(hit, 1.0, 0.0).astype(F32))
    for b in range(block_count):
        part = pl.ds(b * block_rows, block_rows)
        v = pre[part, :]
        act[part, :] = (v * jax.nn.sigmoid(v) * gates[b]).astype(BF16)

    local[2].wait()
    tile_d = 512

    @pl.loop(0, width // tile_d)
    def _(k):
        cols = pl.ds(pl.multiple_of(k * tile_d, tile_d), tile_d)
        term = jnp.dot(act[...], decw[:, cols], preferred_element_type=F32)
        PT[:, :, cols] = term.astype(BF16).reshape(G.shape[0], rows, tile_d)

    at = 0
    for dx in (1, 0):
        for dz in Z_ORDER + (0,):
            s = lat_of(dz, dx, 1)
            push(PT.at[s], CR.at[s // NC], r_send.at[at], cr_recv.at[s // NC], c_peer)
            at += 1
    push(act, act_o, small_send.at[0], small_recv.at[0], y_peer)

    def add_into(dst, *terms):
        @pl.loop(0, width // tile)
        def _(k):
            cols = pl.ds(pl.multiple_of(k * tile, tile), tile)
            total = terms[0][:, cols].astype(F32)
            for term in terms[1:]:
                total = total + term[:, cols].astype(F32)
            dst[:, cols] = total.astype(BF16)

    for dz in Z_ORDER + (0,):
        s = lat_of(dz, 1, 0)
        zz = lax.rem(z + dz, NZ)
        arrived(CR.at[s // NC], r_send.at[0], cr_recv.at[s // NC])
        add_into(XS.at[zz], PT.at[s], CR.at[s // NC])
        push(XS.at[zz], XR.at[zz], r_send.at[at], xr_recv.at[zz], x_peer)
        at += 1
    for dz in Z_ORDER:
        s = lat_of(dz, 0, 0)
        zz = lax.rem(z + dz, NZ)
        arrived(CR.at[s // NC], r_send.at[0], cr_recv.at[s // NC])
        arrived(XR.at[zz], r_send.at[0], xr_recv.at[zz])
        add_into(ZS.at[zz], PT.at[s], CR.at[s // NC], XR.at[zz])
        push(ZS.at[zz], ZR.at[z], r_send.at[at], zr_recv.at[z], z_peer[dz])
        at += 1

    toks.relay_other()
    toks.settle_other()
    arrived(act_o, small_send.at[0], small_recv.at[0])
    out = [
        pltpu.make_async_copy(G.at[:, :, mine], toks_out.at[0], local_sem.at[3]),
        pltpu.make_async_copy(O, toks_out.at[1], local_sem.at[4]),
        pltpu.make_async_copy(act, acts_out.at[0], local_sem.at[5]),
        pltpu.make_async_copy(act_o, acts_out.at[1], local_sem.at[6]),
    ]
    for copy in out:
        copy.start()

    arrived(CR.at[own // NC], r_send.at[0], cr_recv.at[own // NC])
    arrived(XR.at[z], r_send.at[0], xr_recv.at[z])
    for dz in Z_ORDER:
        zz = lax.rem(z + dz, NZ)
        arrived(ZR.at[zz], r_send.at[0], zr_recv.at[zz])

    @pl.loop(0, width // tile)
    def _(k):
        cols = pl.ds(pl.multiple_of(k * tile, tile), tile)
        total = PT[own, :, cols].astype(F32) + CR[own // NC, :, cols].astype(F32)
        total = total + XR[z, :, cols].astype(F32)
        for dz in Z_ORDER:
            total = total + ZR[lax.rem(z + dz, NZ), :, cols].astype(F32)
        total = total + decb_ref[:, cols]
        recon_ref[:, cols] = total.astype(BF16)
        C[own, :, cols] = ((total - G[own, :, cols].astype(F32)) * cot_scale).astype(BF16)

    cots = Gather(C, CO, c_send, c_recv, co_recv)
    cots.spread()
    cots.relay_other()
    cots.settle()

    for b in range(block_count):
        part = pl.ds(b * block_rows, block_rows)
        v = pre[part, :]
        sigma = jax.nn.sigmoid(v)
        pre[part, :] = sigma * (1.0 + v * (1.0 - sigma)) * gates[b]
    grad = jnp.zeros((group_rows, lat_width), F32)

    def grad_step(k, grad):
        cols = pl.ds(pl.multiple_of(k * tile, tile), tile)
        return grad + lax.dot_general(
            C[:, :, cols].reshape(group_rows, tile), decw[:, cols],
            (((1,), (1,)), ((), ())), preferred_element_type=F32,
        )

    grad = lax.fori_loop(0, width // tile, grad_step, grad)
    pg[...] = (grad * pre[...]).astype(BF16)
    push(pg, pg_o, small_send.at[1], small_recv.at[1], y_peer)
    out.append(pltpu.make_async_copy(C.at[:, :, mine], cots_out.at[0], local_sem.at[7]))
    out[-1].start()
    cots.settle_other()
    out.append(pltpu.make_async_copy(CO, cots_out.at[1], local_sem.at[8]))
    out[-1].start()
    out.append(pltpu.make_async_copy(pg, grads_out.at[0], local_sem.at[9]))
    out[-1].start()
    arrived(pg_o, small_send.at[1], small_recv.at[1])
    out.append(pltpu.make_async_copy(pg_o, grads_out.at[1], local_sem.at[10]))
    out[-1].start()
    for copy in sent:
        copy.wait_send()
    for copy in out:
        copy.wait()


def fused_shards(tokens, enc_weight, enc_bias, dec_weight, dec_bias, active_blocks):
    rows, width = tokens.shape
    lat_count = lax.axis_size("lat")
    tok_count = lax.axis_size("tok")
    group_rows = rows * lat_count
    latents = enc_weight.shape[1]
    half = width // tok_count
    cot_scale = 1.0 / math.sqrt(group_rows * tok_count)
    hbm = pl.BlockSpec(memory_space=pl.ANY)
    vmem = pl.BlockSpec(memory_space=pltpu.VMEM)
    dma = pltpu.SemaphoreType.DMA
    recon, toks, cots, acts, grads = pl.pallas_call(
        functools.partial(fused_kernel, cot_scale),
        out_shape=(
            jax.ShapeDtypeStruct((rows, width), BF16),
            jax.ShapeDtypeStruct((2, lat_count, rows, half), BF16),
            jax.ShapeDtypeStruct((2, lat_count, rows, half), BF16),
            jax.ShapeDtypeStruct((2, group_rows, latents), BF16),
            jax.ShapeDtypeStruct((2, group_rows, latents), BF16),
        ),
        in_specs=[hbm, hbm, vmem, hbm, vmem, pl.BlockSpec(memory_space=pltpu.SMEM)],
        out_specs=(vmem, hbm, hbm, hbm, hbm),
        scratch_shapes=[
            pltpu.VMEM((width, latents), BF16),
            pltpu.VMEM((latents, width), BF16),
            pltpu.VMEM((lat_count, rows, width), BF16),
            pltpu.VMEM((lat_count, rows, half), BF16),
            pltpu.VMEM((lat_count, rows, width), BF16),
            pltpu.VMEM((lat_count, rows, half), BF16),
            pltpu.VMEM((lat_count, rows, width), BF16),
            pltpu.VMEM((lat_count // NC, rows, width), BF16),
            pltpu.VMEM((NZ, rows, width), BF16),
            pltpu.VMEM((NZ, rows, width), BF16),
            pltpu.VMEM((NZ, rows, width), BF16),
            pltpu.VMEM((NZ, rows, width), BF16),
            pltpu.VMEM((group_rows, latents), F32),
            pltpu.VMEM((group_rows, latents), BF16),
            pltpu.VMEM((group_rows, latents), BF16),
            pltpu.VMEM((group_rows, latents), BF16),
            pltpu.VMEM((group_rows, latents), BF16),
            dma((11,)),
            dma((32,)), dma((16,)), dma((16,)),
            dma((32,)), dma((16,)), dma((16,)),
            dma((15,)), dma((8,)), dma((4,)), dma((4,)),
            dma((2,)), dma((2,)),
        ],
        compiler_params=pltpu.CompilerParams(
            collective_id=0, has_side_effects=True, vmem_limit_bytes=56 * 1024 * 1024
        ),
        name="fused_step",
    )(tokens, enc_weight, enc_bias[None, :], dec_weight, dec_bias[None, :], active_blocks)
    enc_grad = contract_rows(toks.reshape(2 * group_rows, half), grads.reshape(2 * group_rows, latents))
    dec_grad = contract_rows(acts.reshape(2 * group_rows, latents), cots.reshape(2 * group_rows, half))
    return recon, enc_grad, dec_grad


def shards(tokens, enc_weight, enc_bias, dec_weight, dec_bias, active_blocks):
    tok_dev = tokens.shape[0]
    lat_count = lax.axis_size("lat")
    tok_count = lax.axis_size("tok")
    group_rows = tok_dev * lat_count
    latent_width = enc_weight.shape[1]
    block_count = active_blocks.shape[0]
    block_rows = group_rows // block_count
    blocks_here = latent_width // LB
    owner_index = lax.axis_index("lat")
    cot_scale = 1.0 / math.sqrt(group_rows * tok_count)
    block_ids = owner_index * blocks_here + jnp.arange(blocks_here, dtype=jnp.int32)
    block_hits = jnp.any(active_blocks[:, :, None] == block_ids[None, None, :], axis=1).astype(
        jnp.float32
    )
    latent_gate = jnp.repeat(block_hits, LB, axis=1)[:, None, :]
    bias_row = enc_bias[None, None, :]
    gathered = lax.all_gather(tokens, "lat", axis=0, tiled=True)
    pre_act = (
        jnp.dot(gathered, enc_weight, preferred_element_type=jnp.float32).reshape(
            block_count, block_rows, latent_width
        )
        + bias_row
    )
    activations = (
        (jax.nn.silu(pre_act) * latent_gate).astype(jnp.bfloat16).reshape(group_rows, latent_width)
    )
    bias_dec = dec_bias[None, :]
    partial_sum = jnp.dot(activations, dec_weight, preferred_element_type=jnp.float32)
    decoded_all = lax.psum(partial_sum.astype(jnp.bfloat16), "lat").astype(jnp.float32) + bias_dec
    cot_all = ((decoded_all - gathered.astype(jnp.float32)) * cot_scale).astype(jnp.bfloat16)
    decoded = lax.dynamic_slice_in_dim(decoded_all, owner_index * tok_dev, tok_dev, 0)
    dec_local = contract_rows(activations, cot_all)
    latent_grad = lax.dot_general(
        cot_all, dec_weight, (((1,), (1,)), ((), ())), preferred_element_type=jnp.float32
    )
    sigma = jax.nn.sigmoid(pre_act)
    slope = sigma * (1.0 + pre_act * (1.0 - sigma))
    pre_grad = (
        (latent_grad.reshape(block_count, block_rows, latent_width) * slope * latent_gate)
        .astype(jnp.bfloat16)
        .reshape(group_rows, latent_width)
    )
    enc_local = contract_rows(gathered, pre_grad)
    enc_grad, dec_grad = (
        lax.psum_scatter(
            enc_local.astype(jnp.bfloat16), "tok", scatter_dimension=0, tiled=True
        ).astype(jnp.float32),
        lax.psum_scatter(
            dec_local.astype(jnp.bfloat16), "tok", scatter_dimension=1, tiled=True
        ).astype(jnp.float32),
    )
    return (decoded.astype(jnp.bfloat16), enc_grad, dec_grad)


def solution(mesh):
    placed = (
        P(("tok", "lat"), None),
        P(None, "lat"),
        P("lat"),
        P("lat", None),
        P(),
        P("tok", None),
    )
    fits = mesh.shape["tok"] == 2 and mesh.shape["lat"] == NZ * NX * NC
    return jax.shard_map(
        fused_shards if fits else shards,
        mesh=mesh,
        in_specs=placed,
        out_specs=(P(("tok", "lat"), None), P("tok", "lat"), P("lat", "tok")),
        check_vma=False,
    )
```

```python
import functools
import math

import jax
import jax.numpy as jnp
from jax import lax
from jax.experimental import pallas as pl
from jax.experimental.pallas import tpu as pltpu
from jax.sharding import PartitionSpec as P

LB = 256
MESH = pl.DeviceIdType.MESH
NZ, NX, NC = 4, 2, 2
Z_ORDER = (2, 1, 3)
BF16 = jnp.bfloat16
F32 = jnp.float32


def contract_rows(left_rows, right_rows):
    return lax.dot_general(
        left_rows, right_rows, (((0,), (0,)), ((), ())), preferred_element_type=jnp.float32
    )


def fused_kernel(
    cot_scale,
    tok_hbm, encw_hbm, encb_ref, decw_hbm, decb_ref, blocks_ref,
    recon_ref, toks_out, cots_out, acts_out, grads_out,
    encw, decw, G, O, C, CO, PT, CR, XS, XR, ZS, ZR, pre, act, act_o, pg, pg_o,
    local_sem, g_send, g_recv, o_recv, c_send, c_recv, co_recv,
    r_send, cr_recv, xr_recv, zr_recv, small_send, small_recv,
):
    t = lax.axis_index("tok")
    l = lax.axis_index("lat")
    z, x, c = l // (NX * NC), (l // NC) % NX, l % NC
    rows, width = tok_hbm.shape
    half = width // 2

    def lat_of(dz, dx, dc):
        zz = lax.rem(z + dz, NZ)
        xx = x if dx == 0 else 1 - x
        cc = c if dc == 0 else 1 - c
        return (zz * NX + xx) * NC + cc

    def shard(zz, xx, cc):
        return (zz * NX + xx) * NC + cc

    own = lat_of(0, 0, 0)
    sources = (z + 1 - 2 * lax.rem(z, 2), 2 - z // 2, 3 - 3 * (z // 2))
    interior = jnp.logical_and(z >= 1, z <= 2)
    pair, inner = (t, shard(sources[0], x, c)), (t, shard(3 - z, x, c))
    z_peer = {dz: (t, lat_of(dz, 0, 0)) for dz in Z_ORDER}
    x_peer = (t, lat_of(0, 1, 0))
    c_peer = (t, lat_of(0, 0, 1))
    y_peer = (1 - t, l)

    local = [
        pltpu.make_async_copy(tok_hbm, G.at[own], local_sem.at[0]),
        pltpu.make_async_copy(encw_hbm, encw, local_sem.at[1]),
        pltpu.make_async_copy(decw_hbm, decw, local_sem.at[2]),
    ]
    for copy in local:
        copy.start()

    barrier = pltpu.get_barrier_semaphore()
    peers = [z_peer[dz] for dz in Z_ORDER] + [x_peer, c_peer, y_peer]
    for peer in peers:
        pl.semaphore_signal(barrier, inc=1, device_id=peer, device_id_type=MESH)
    pl.semaphore_wait(barrier, len(peers))

    sent = []

    def push(src, dst, send_sem, recv_sem, peer, when=None):
        copy = pltpu.make_async_remote_copy(
            src_ref=src, dst_ref=dst, send_sem=send_sem, recv_sem=recv_sem,
            device_id=peer, device_id_type=MESH,
        )
        if when is None:
            copy.start()
        else:
            pl.when(when)(lambda: copy.start())
        sent.append((copy, when))

    def arrived(dst, send_sem, recv_sem):
        pltpu.make_async_remote_copy(
            src_ref=dst, dst_ref=dst, send_sem=send_sem, recv_sem=recv_sem,
            device_id=c_peer, device_id_type=MESH,
        ).wait_recv()

    mine = pl.ds(pl.multiple_of(t * half, half), half)
    theirs = pl.ds(pl.multiple_of((1 - t) * half, half), half)

    class Gather:
        def __init__(self, full, other, send, recv, other_recv):
            self.full, self.other = full, other
            self.send, self.recv, self.other_recv = send, recv, other_recv
            self.count = 0

        def next_send(self):
            self.count += 1
            return self.send.at[self.count - 1]

        def piece(self, s, h):
            ref = self.full.at[s, :, theirs if h == 0 else mine]
            return ref, self.recv.at[s * 2 + h]

        def give(self, peer, s, h, when=None):
            ref, sem = self.piece(s, h)
            push(ref, ref, self.next_send(), sem, peer, when)

        def give_y(self, s):
            push(
                self.full.at[s, :, theirs], self.other.at[s], self.next_send(),
                self.other_recv.at[s], y_peer,
            )

        def take(self, s, h):
            ref, sem = self.piece(s, h)
            arrived(ref, self.send.at[0], sem)

        def spread(self):
            self.give(pair, own, 0)
            self.give(inner, own, 0, interior)
            self.give(x_peer, own, 0)
            self.give_y(own)
            self.give(pair, own, 1)
            self.give(inner, own, 1, interior)
            self.give(x_peer, own, 1)
            self.give(c_peer, own, 0)
            self.give(c_peer, own, 1)

            def from_z(i, h):
                s = shard(sources[i], x, c)
                self.take(s, h)
                self.give(inner if i == 0 else pair, s, h, interior)
                self.give(x_peer, s, h)
                if h == 0:
                    self.give_y(s)
                self.give(c_peer, s, h)

            def from_x(zz, h):
                s = shard(zz, 1 - x, c)
                self.take(s, h)
                if h == 0:
                    self.give_y(s)
                self.give(c_peer, s, h)

            behind = z
            for i in range(NZ - 1):
                for h in range(2):
                    from_z(i, h)
                    from_x(behind, h)
                behind = sources[i]
            for h in range(2):
                from_x(behind, h)

        def relay_other(self):
            order = [(z, x), (sources[0], x), (z, 1 - x)]
            order += [(sources[1], x), (sources[0], 1 - x), (sources[2], x)]
            order += [(sources[1], 1 - x), (sources[2], 1 - x)]
            for zz, xx in order:
                s = shard(zz, xx, c)
                arrived(self.other.at[s], self.send.at[0], self.other_recv.at[s])
                push(
                    self.other.at[s], self.other.at[s], self.next_send(),
                    self.other_recv.at[s], c_peer,
                )

        def settle(self):
            for dx in range(NX):
                for dz in (0,) + Z_ORDER:
                    for h in range(2):
                        self.take(lat_of(dz, dx, 1), h)

        def settle_other(self):
            for dx in range(NX):
                for dz in (0,) + Z_ORDER:
                    s = lat_of(dz, dx, 1)
                    arrived(self.other.at[s], self.send.at[0], self.other_recv.at[s])

    local[0].wait()
    toks = Gather(G, O, g_send, g_recv, o_recv)
    toks.spread()
    toks.settle()

    group_rows = G.shape[0] * rows
    lat_width = encw.shape[1]
    local[1].wait()
    tile = 1024
    pre[...] = jnp.broadcast_to(encb_ref[...], pre.shape)

    @pl.loop(0, width // tile)
    def _(k):
        cols = pl.ds(pl.multiple_of(k * tile, tile), tile)
        pre[...] += jnp.dot(
            G[:, :, cols].reshape(group_rows, tile), encw[cols, :], preferred_element_type=F32
        )

    block_count = blocks_ref.shape[0]
    block_rows = group_rows // block_count
    gates = []
    for b in range(block_count):
        hit = blocks_ref[b, 0] == l
        for slot in range(1, blocks_ref.shape[1]):
            hit = jnp.logical_or(hit, blocks_ref[b, slot] == l)
        gates.append(jnp.where(hit, 1.0, 0.0).astype(F32))
    for b in range(block_count):
        part = pl.ds(b * block_rows, block_rows)
        v = pre[part, :]
        act[part, :] = (v * jax.nn.sigmoid(v) * gates[b]).astype(BF16)

    local[2].wait()
    tile_d = 512

    @pl.loop(0, width // tile_d)
    def _(k):
        cols = pl.ds(pl.multiple_of(k * tile_d, tile_d), tile_d)
        term = jnp.dot(act[...], decw[:, cols], preferred_element_type=F32)
        PT[:, :, cols] = term.astype(BF16).reshape(G.shape[0], rows, tile_d)

    at = 0
    for dx in (1, 0):
        for dz in Z_ORDER + (0,):
            s = lat_of(dz, dx, 1)
            push(PT.at[s], CR.at[s // NC], r_send.at[at], cr_recv.at[s // NC], c_peer)
            at += 1
    push(act, act_o, small_send.at[0], small_recv.at[0], y_peer)

    def add_into(dst, *terms):
        @pl.loop(0, width // tile)
        def _(k):
            cols = pl.ds(pl.multiple_of(k * tile, tile), tile)
            total = terms[0][:, cols].astype(F32)
            for term in terms[1:]:
                total = total + term[:, cols].astype(F32)
            dst[:, cols] = total.astype(BF16)

    for dz in Z_ORDER + (0,):
        s = lat_of(dz, 1, 0)
        zz = lax.rem(z + dz, NZ)
        arrived(CR.at[s // NC], r_send.at[0], cr_recv.at[s // NC])
        add_into(XS.at[zz], PT.at[s], CR.at[s // NC])
        push(XS.at[zz], XR.at[zz], r_send.at[at], xr_recv.at[zz], x_peer)
        at += 1
    for dz in Z_ORDER:
        s = lat_of(dz, 0, 0)
        zz = lax.rem(z + dz, NZ)
        arrived(CR.at[s // NC], r_send.at[0], cr_recv.at[s // NC])
        arrived(XR.at[zz], r_send.at[0], xr_recv.at[zz])
        add_into(ZS.at[zz], PT.at[s], CR.at[s // NC], XR.at[zz])
        push(ZS.at[zz], ZR.at[z], r_send.at[at], zr_recv.at[z], z_peer[dz])
        at += 1

    toks.relay_other()
    toks.settle_other()
    arrived(act_o, small_send.at[0], small_recv.at[0])
    out = [
        pltpu.make_async_copy(G.at[:, :, mine], toks_out.at[0], local_sem.at[3]),
        pltpu.make_async_copy(O, toks_out.at[1], local_sem.at[4]),
        pltpu.make_async_copy(act, acts_out.at[0], local_sem.at[5]),
        pltpu.make_async_copy(act_o, acts_out.at[1], local_sem.at[6]),
    ]
    for copy in out:
        copy.start()

    arrived(CR.at[own // NC], r_send.at[0], cr_recv.at[own // NC])
    arrived(XR.at[z], r_send.at[0], xr_recv.at[z])
    for dz in Z_ORDER:
        zz = lax.rem(z + dz, NZ)
        arrived(ZR.at[zz], r_send.at[0], zr_recv.at[zz])

    @pl.loop(0, width // tile)
    def _(k):
        cols = pl.ds(pl.multiple_of(k * tile, tile), tile)
        total = PT[own, :, cols].astype(F32) + CR[own // NC, :, cols].astype(F32)
        total = total + XR[z, :, cols].astype(F32)
        for dz in Z_ORDER:
            total = total + ZR[lax.rem(z + dz, NZ), :, cols].astype(F32)
        total = total + decb_ref[:, cols]
        recon_ref[:, cols] = total.astype(BF16)
        C[own, :, cols] = ((total - G[own, :, cols].astype(F32)) * cot_scale).astype(BF16)

    cots = Gather(C, CO, c_send, c_recv, co_recv)
    cots.spread()
    cots.settle()

    for b in range(block_count):
        part = pl.ds(b * block_rows, block_rows)
        v = pre[part, :]
        sigma = jax.nn.sigmoid(v)
        pre[part, :] = sigma * (1.0 + v * (1.0 - sigma)) * gates[b]
    grad = jnp.zeros((group_rows, lat_width), F32)

    def grad_step(k, grad):
        cols = pl.ds(pl.multiple_of(k * tile, tile), tile)
        return grad + lax.dot_general(
            C[:, :, cols].reshape(group_rows, tile), decw[:, cols],
            (((1,), (1,)), ((), ())), preferred_element_type=F32,
        )

    grad = lax.fori_loop(0, width // tile, grad_step, grad)
    pg[...] = (grad * pre[...]).astype(BF16)
    push(pg, pg_o, small_send.at[1], small_recv.at[1], y_peer)
    out.append(pltpu.make_async_copy(C.at[:, :, mine], cots_out.at[0], local_sem.at[7]))
    out[-1].start()
    cots.relay_other()
    cots.settle_other()
    out.append(pltpu.make_async_copy(CO, cots_out.at[1], local_sem.at[8]))
    out[-1].start()
    out.append(pltpu.make_async_copy(pg, grads_out.at[0], local_sem.at[9]))
    out[-1].start()
    arrived(pg_o, small_send.at[1], small_recv.at[1])
    out.append(pltpu.make_async_copy(pg_o, grads_out.at[1], local_sem.at[10]))
    out[-1].start()
    for copy, when in sent:
        if when is None:
            copy.wait_send()
        else:
            pl.when(when)(lambda: copy.wait_send())
    for copy in out:
        copy.wait()


def fused_shards(tokens, enc_weight, enc_bias, dec_weight, dec_bias, active_blocks):
    rows, width = tokens.shape
    lat_count = lax.axis_size("lat")
    tok_count = lax.axis_size("tok")
    group_rows = rows * lat_count
    latents = enc_weight.shape[1]
    half = width // tok_count
    cot_scale = 1.0 / math.sqrt(group_rows * tok_count)
    hbm = pl.BlockSpec(memory_space=pl.ANY)
    vmem = pl.BlockSpec(memory_space=pltpu.VMEM)
    dma = pltpu.SemaphoreType.DMA
    recon, toks, cots, acts, grads = pl.pallas_call(
        functools.partial(fused_kernel, cot_scale),
        out_shape=(
            jax.ShapeDtypeStruct((rows, width), BF16),
            jax.ShapeDtypeStruct((2, lat_count, rows, half), BF16),
            jax.ShapeDtypeStruct((2, lat_count, rows, half), BF16),
            jax.ShapeDtypeStruct((2, group_rows, latents), BF16),
            jax.ShapeDtypeStruct((2, group_rows, latents), BF16),
        ),
        in_specs=[hbm, hbm, vmem, hbm, vmem, pl.BlockSpec(memory_space=pltpu.SMEM)],
        out_specs=(vmem, hbm, hbm, hbm, hbm),
        scratch_shapes=[
            pltpu.VMEM((width, latents), BF16),
            pltpu.VMEM((latents, width), BF16),
            pltpu.VMEM((lat_count, rows, width), BF16),
            pltpu.VMEM((lat_count, rows, half), BF16),
            pltpu.VMEM((lat_count, rows, width), BF16),
            pltpu.VMEM((lat_count, rows, half), BF16),
            pltpu.VMEM((lat_count, rows, width), BF16),
            pltpu.VMEM((lat_count // NC, rows, width), BF16),
            pltpu.VMEM((NZ, rows, width), BF16),
            pltpu.VMEM((NZ, rows, width), BF16),
            pltpu.VMEM((NZ, rows, width), BF16),
            pltpu.VMEM((NZ, rows, width), BF16),
            pltpu.VMEM((group_rows, latents), F32),
            pltpu.VMEM((group_rows, latents), BF16),
            pltpu.VMEM((group_rows, latents), BF16),
            pltpu.VMEM((group_rows, latents), BF16),
            pltpu.VMEM((group_rows, latents), BF16),
            dma((11,)),
            dma((50,)), dma((32,)), dma((16,)),
            dma((50,)), dma((32,)), dma((16,)),
            dma((15,)), dma((8,)), dma((4,)), dma((4,)),
            dma((2,)), dma((2,)),
        ],
        compiler_params=pltpu.CompilerParams(
            collective_id=0, has_side_effects=True, vmem_limit_bytes=56 * 1024 * 1024
        ),
        name="fused_step",
    )(tokens, enc_weight, enc_bias[None, :], dec_weight, dec_bias[None, :], active_blocks)
    enc_grad = contract_rows(toks.reshape(2 * group_rows, half), grads.reshape(2 * group_rows, latents))
    dec_grad = contract_rows(acts.reshape(2 * group_rows, latents), cots.reshape(2 * group_rows, half))
    return recon, enc_grad, dec_grad


def shards(tokens, enc_weight, enc_bias, dec_weight, dec_bias, active_blocks):
    tok_dev = tokens.shape[0]
    lat_count = lax.axis_size("lat")
    tok_count = lax.axis_size("tok")
    group_rows = tok_dev * lat_count
    latent_width = enc_weight.shape[1]
    block_count = active_blocks.shape[0]
    block_rows = group_rows // block_count
    blocks_here = latent_width // LB
    owner_index = lax.axis_index("lat")
    cot_scale = 1.0 / math.sqrt(group_rows * tok_count)
    block_ids = owner_index * blocks_here + jnp.arange(blocks_here, dtype=jnp.int32)
    block_hits = jnp.any(active_blocks[:, :, None] == block_ids[None, None, :], axis=1).astype(
        jnp.float32
    )
    latent_gate = jnp.repeat(block_hits, LB, axis=1)[:, None, :]
    bias_row = enc_bias[None, None, :]
    gathered = lax.all_gather(tokens, "lat", axis=0, tiled=True)
    pre_act = (
        jnp.dot(gathered, enc_weight, preferred_element_type=jnp.float32).reshape(
            block_count, block_rows, latent_width
        )
        + bias_row
    )
    activations = (
        (jax.nn.silu(pre_act) * latent_gate).astype(jnp.bfloat16).reshape(group_rows, latent_width)
    )
    bias_dec = dec_bias[None, :]
    partial_sum = jnp.dot(activations, dec_weight, preferred_element_type=jnp.float32)
    decoded_all = lax.psum(partial_sum.astype(jnp.bfloat16), "lat").astype(jnp.float32) + bias_dec
    cot_all = ((decoded_all - gathered.astype(jnp.float32)) * cot_scale).astype(jnp.bfloat16)
    decoded = lax.dynamic_slice_in_dim(decoded_all, owner_index * tok_dev, tok_dev, 0)
    dec_local = contract_rows(activations, cot_all)
    latent_grad = lax.dot_general(
        cot_all, dec_weight, (((1,), (1,)), ((), ())), preferred_element_type=jnp.float32
    )
    sigma = jax.nn.sigmoid(pre_act)
    slope = sigma * (1.0 + pre_act * (1.0 - sigma))
    pre_grad = (
        (latent_grad.reshape(block_count, block_rows, latent_width) * slope * latent_gate)
        .astype(jnp.bfloat16)
        .reshape(group_rows, latent_width)
    )
    enc_local = contract_rows(gathered, pre_grad)
    enc_grad, dec_grad = (
        lax.psum_scatter(
            enc_local.astype(jnp.bfloat16), "tok", scatter_dimension=0, tiled=True
        ).astype(jnp.float32),
        lax.psum_scatter(
            dec_local.astype(jnp.bfloat16), "tok", scatter_dimension=1, tiled=True
        ).astype(jnp.float32),
    )
    return (decoded.astype(jnp.bfloat16), enc_grad, dec_grad)


def solution(mesh):
    placed = (
        P(("tok", "lat"), None),
        P(None, "lat"),
        P("lat"),
        P("lat", None),
        P(),
        P("tok", None),
    )
    fits = mesh.shape["tok"] == 2 and mesh.shape["lat"] == NZ * NX * NC
    return jax.shard_map(
        fused_shards if fits else shards,
        mesh=mesh,
        in_specs=placed,
        out_specs=(P(("tok", "lat"), None), P("tok", "lat"), P("lat", "tok")),
        check_vma=False,
    )
```

```python
import functools
import math

import jax
import jax.numpy as jnp
from jax import lax
from jax.experimental import pallas as pl
from jax.experimental.pallas import tpu as pltpu
from jax.sharding import PartitionSpec as P

LB = 256
MESH = pl.DeviceIdType.MESH
NZ, NX, NC = 4, 2, 2
Z_ORDER = (2, 1, 3)
BF16 = jnp.bfloat16
F32 = jnp.float32


def contract_rows(left_rows, right_rows):
    return lax.dot_general(
        left_rows, right_rows, (((0,), (0,)), ((), ())), preferred_element_type=jnp.float32
    )


def fused_kernel(
    cot_scale,
    tok_hbm, encw_hbm, encb_ref, decw_hbm, decb_ref, blocks_ref,
    recon_ref, toks_out, cots_out, acts_out, grads_out,
    encw, decw, G, O, C, CO, PT, CR, XS, XR, ZS, ZR, pre, act, act_o, pg, pg_o,
    local_sem, g_send, g_recv, o_recv, c_send, c_recv, co_recv,
    r_send, cr_recv, xr_recv, zr_recv, small_send, small_recv,
):
    t = lax.axis_index("tok")
    l = lax.axis_index("lat")
    z, x, c = l // (NX * NC), (l // NC) % NX, l % NC
    rows, width = tok_hbm.shape
    half = width // 2

    def lat_of(dz, dx, dc):
        zz = lax.rem(z + dz, NZ)
        xx = x if dx == 0 else 1 - x
        cc = c if dc == 0 else 1 - c
        return (zz * NX + xx) * NC + cc

    def shard(zz, xx, cc):
        return (zz * NX + xx) * NC + cc

    own = lat_of(0, 0, 0)
    sources = (z + 1 - 2 * lax.rem(z, 2), 2 - z // 2, 3 - 3 * (z // 2))
    interior = jnp.logical_and(z >= 1, z <= 2)
    pair, inner = (t, shard(sources[0], x, c)), (t, shard(3 - z, x, c))
    z_peer = {dz: (t, lat_of(dz, 0, 0)) for dz in Z_ORDER}
    x_peer = (t, lat_of(0, 1, 0))
    c_peer = (t, lat_of(0, 0, 1))
    y_peer = (1 - t, l)

    local = [
        pltpu.make_async_copy(tok_hbm, G.at[own], local_sem.at[0]),
        pltpu.make_async_copy(encw_hbm, encw, local_sem.at[1]),
        pltpu.make_async_copy(decw_hbm, decw, local_sem.at[2]),
    ]
    for copy in local:
        copy.start()

    barrier = pltpu.get_barrier_semaphore()
    peers = [z_peer[dz] for dz in Z_ORDER] + [x_peer, c_peer, y_peer]
    for peer in peers:
        pl.semaphore_signal(barrier, inc=1, device_id=peer, device_id_type=MESH)
    pl.semaphore_wait(barrier, len(peers))

    sent = []

    def push(src, dst, send_sem, recv_sem, peer, when=None):
        copy = pltpu.make_async_remote_copy(
            src_ref=src, dst_ref=dst, send_sem=send_sem, recv_sem=recv_sem,
            device_id=peer, device_id_type=MESH,
        )
        if when is None:
            copy.start()
        else:
            pl.when(when)(lambda: copy.start())
        sent.append((copy, when))

    def arrived(dst, send_sem, recv_sem):
        pltpu.make_async_remote_copy(
            src_ref=dst, dst_ref=dst, send_sem=send_sem, recv_sem=recv_sem,
            device_id=c_peer, device_id_type=MESH,
        ).wait_recv()

    mine = pl.ds(pl.multiple_of(t * half, half), half)
    theirs = pl.ds(pl.multiple_of((1 - t) * half, half), half)

    class Gather:
        def __init__(self, full, other, send, recv, other_recv):
            self.full, self.other = full, other
            self.send, self.recv, self.other_recv = send, recv, other_recv
            self.count = 0

        def next_send(self):
            self.count += 1
            return self.send.at[self.count - 1]

        def piece(self, s, h):
            ref = self.full.at[s, :, theirs if h == 0 else mine]
            return ref, self.recv.at[s * 2 + h]

        def give(self, peer, s, h, when=None):
            ref, sem = self.piece(s, h)
            push(ref, ref, self.next_send(), sem, peer, when)

        def give_y(self, s):
            push(
                self.full.at[s, :, theirs], self.other.at[s], self.next_send(),
                self.other_recv.at[s], y_peer,
            )

        def take(self, s, h):
            ref, sem = self.piece(s, h)
            arrived(ref, self.send.at[0], sem)

        def spread(self):
            self.give(pair, own, 0)
            self.give(inner, own, 0, interior)
            self.give(x_peer, own, 0)
            self.give_y(own)
            self.give(pair, own, 1)
            self.give(inner, own, 1, interior)
            self.give(x_peer, own, 1)
            self.give(c_peer, own, 0)
            self.give(c_peer, own, 1)

            def from_z(i, h):
                s = shard(sources[i], x, c)
                self.take(s, h)
                self.give(inner if i == 0 else pair, s, h, interior)
                self.give(x_peer, s, h)
                if h == 0:
                    self.give_y(s)
                self.give(c_peer, s, h)

            def from_x(zz, h):
                s = shard(zz, 1 - x, c)
                self.take(s, h)
                if h == 0:
                    self.give_y(s)
                self.give(c_peer, s, h)

            behind = z
            for i in range(NZ - 1):
                for h in range(2):
                    from_z(i, h)
                    from_x(behind, h)
                behind = sources[i]
            for h in range(2):
                from_x(behind, h)

        def relay_other(self):
            order = [(z, x), (sources[0], x), (z, 1 - x)]
            order += [(sources[1], x), (sources[0], 1 - x), (sources[2], x)]
            order += [(sources[1], 1 - x), (sources[2], 1 - x)]
            for zz, xx in order:
                s = shard(zz, xx, c)
                arrived(self.other.at[s], self.send.at[0], self.other_recv.at[s])
                push(
                    self.other.at[s], self.other.at[s], self.next_send(),
                    self.other_recv.at[s], c_peer,
                )

        def settle(self):
            for dx in range(NX):
                for dz in (0,) + Z_ORDER:
                    for h in range(2):
                        self.take(lat_of(dz, dx, 1), h)

        def settle_other(self):
            for dx in range(NX):
                for dz in (0,) + Z_ORDER:
                    s = lat_of(dz, dx, 1)
                    arrived(self.other.at[s], self.send.at[0], self.other_recv.at[s])

    local[0].wait()
    toks = Gather(G, O, g_send, g_recv, o_recv)
    toks.spread()
    toks.settle()

    group_rows = G.shape[0] * rows
    lat_width = encw.shape[1]
    local[1].wait()
    tile = 1024
    pre[...] = jnp.broadcast_to(encb_ref[...], pre.shape)

    @pl.loop(0, width // tile)
    def _(k):
        cols = pl.ds(pl.multiple_of(k * tile, tile), tile)
        pre[...] += jnp.dot(
            G[:, :, cols].reshape(group_rows, tile), encw[cols, :], preferred_element_type=F32
        )

    block_count = blocks_ref.shape[0]
    block_rows = group_rows // block_count
    gates = []
    for b in range(block_count):
        hit = blocks_ref[b, 0] == l
        for slot in range(1, blocks_ref.shape[1]):
            hit = jnp.logical_or(hit, blocks_ref[b, slot] == l)
        gates.append(jnp.where(hit, 1.0, 0.0).astype(F32))
    for b in range(block_count):
        part = pl.ds(b * block_rows, block_rows)
        v = pre[part, :]
        act[part, :] = (v * jax.nn.sigmoid(v) * gates[b]).astype(BF16)

    local[2].wait()
    tile_d = 512
    halves = [pl.ds(h * half, half) for h in range(2)]
    at = 0
    for h in range(2):

        @pl.loop(h * half // tile_d, (h + 1) * half // tile_d)
        def _(k):
            cols = pl.ds(pl.multiple_of(k * tile_d, tile_d), tile_d)
            term = jnp.dot(act[...], decw[:, cols], preferred_element_type=F32)
            PT[:, :, cols] = term.astype(BF16).reshape(G.shape[0], rows, tile_d)

        for dz in Z_ORDER + (0,):
            s = lat_of(dz, 1, 1)
            push(
                PT.at[s, :, halves[h]], CR.at[s // NC, :, halves[h]],
                r_send.at[at], cr_recv.at[s // NC * 2 + h], c_peer,
            )
            at += 1
    for h in range(2):
        for dz in Z_ORDER + (0,):
            s = lat_of(dz, 0, 1)
            push(
                PT.at[s, :, halves[h]], CR.at[s // NC, :, halves[h]],
                r_send.at[at], cr_recv.at[s // NC * 2 + h], c_peer,
            )
            at += 1
    push(act, act_o, small_send.at[0], small_recv.at[0], y_peer)

    def add_into(h, dst, *terms):
        @pl.loop(h * half // tile, (h + 1) * half // tile)
        def _(k):
            cols = pl.ds(pl.multiple_of(k * tile, tile), tile)
            total = terms[0][:, cols].astype(F32)
            for term in terms[1:]:
                total = total + term[:, cols].astype(F32)
            dst[:, cols] = total.astype(BF16)

    def core_in(slot, h):
        arrived(CR.at[slot, :, halves[h]], r_send.at[0], cr_recv.at[slot * 2 + h])

    def x_in(zz, h):
        arrived(XR.at[zz, :, halves[h]], r_send.at[0], xr_recv.at[zz * 2 + h])

    for dz, h in [(dz, h) for h in range(2) for dz in Z_ORDER] + [(0, 0), (0, 1)]:
        s = lat_of(dz, 1, 0)
        zz = lax.rem(z + dz, NZ)
        core_in(s // NC, h)
        add_into(h, XS.at[zz], PT.at[s], CR.at[s // NC])
        push(
            XS.at[zz, :, halves[h]], XR.at[zz, :, halves[h]],
            r_send.at[at], xr_recv.at[zz * 2 + h], x_peer,
        )
        at += 1
    for dz, h in [(dz, h) for h in range(2) for dz in Z_ORDER]:
        s = lat_of(dz, 0, 0)
        zz = lax.rem(z + dz, NZ)
        core_in(s // NC, h)
        x_in(zz, h)
        add_into(h, ZS.at[zz], PT.at[s], CR.at[s // NC], XR.at[zz])
        push(
            ZS.at[zz, :, halves[h]], ZR.at[z, :, halves[h]],
            r_send.at[at], zr_recv.at[z * 2 + h], z_peer[dz],
        )
        at += 1

    toks.relay_other()
    toks.settle_other()
    arrived(act_o, small_send.at[0], small_recv.at[0])
    out = [
        pltpu.make_async_copy(G.at[:, :, mine], toks_out.at[0], local_sem.at[3]),
        pltpu.make_async_copy(O, toks_out.at[1], local_sem.at[4]),
        pltpu.make_async_copy(act, acts_out.at[0], local_sem.at[5]),
        pltpu.make_async_copy(act_o, acts_out.at[1], local_sem.at[6]),
    ]
    for copy in out:
        copy.start()

    for h in range(2):
        core_in(own // NC, h)
        x_in(z, h)
        for dz in Z_ORDER:
            zz = lax.rem(z + dz, NZ)
            arrived(ZR.at[zz, :, halves[h]], r_send.at[0], zr_recv.at[zz * 2 + h])

    @pl.loop(0, width // tile)
    def _(k):
        cols = pl.ds(pl.multiple_of(k * tile, tile), tile)
        total = PT[own, :, cols].astype(F32) + CR[own // NC, :, cols].astype(F32)
        total = total + XR[z, :, cols].astype(F32)
        for dz in Z_ORDER:
            total = total + ZR[lax.rem(z + dz, NZ), :, cols].astype(F32)
        total = total + decb_ref[:, cols]
        recon_ref[:, cols] = total.astype(BF16)
        C[own, :, cols] = ((total - G[own, :, cols].astype(F32)) * cot_scale).astype(BF16)

    cots = Gather(C, CO, c_send, c_recv, co_recv)
    cots.spread()
    cots.settle()

    for b in range(block_count):
        part = pl.ds(b * block_rows, block_rows)
        v = pre[part, :]
        sigma = jax.nn.sigmoid(v)
        pre[part, :] = sigma * (1.0 + v * (1.0 - sigma)) * gates[b]
    grad = jnp.zeros((group_rows, lat_width), F32)

    def grad_step(k, grad):
        cols = pl.ds(pl.multiple_of(k * tile, tile), tile)
        return grad + lax.dot_general(
            C[:, :, cols].reshape(group_rows, tile), decw[:, cols],
            (((1,), (1,)), ((), ())), preferred_element_type=F32,
        )

    grad = lax.fori_loop(0, width // tile, grad_step, grad)
    pg[...] = (grad * pre[...]).astype(BF16)
    push(pg, pg_o, small_send.at[1], small_recv.at[1], y_peer)
    out.append(pltpu.make_async_copy(C.at[:, :, mine], cots_out.at[0], local_sem.at[7]))
    out[-1].start()
    cots.relay_other()
    cots.settle_other()
    out.append(pltpu.make_async_copy(CO, cots_out.at[1], local_sem.at[8]))
    out[-1].start()
    out.append(pltpu.make_async_copy(pg, grads_out.at[0], local_sem.at[9]))
    out[-1].start()
    arrived(pg_o, small_send.at[1], small_recv.at[1])
    out.append(pltpu.make_async_copy(pg_o, grads_out.at[1], local_sem.at[10]))
    out[-1].start()
    for copy, when in sent:
        if when is None:
            copy.wait_send()
        else:
            pl.when(when)(lambda: copy.wait_send())
    for copy in out:
        copy.wait()


def fused_shards(tokens, enc_weight, enc_bias, dec_weight, dec_bias, active_blocks):
    rows, width = tokens.shape
    lat_count = lax.axis_size("lat")
    tok_count = lax.axis_size("tok")
    group_rows = rows * lat_count
    latents = enc_weight.shape[1]
    half = width // tok_count
    cot_scale = 1.0 / math.sqrt(group_rows * tok_count)
    hbm = pl.BlockSpec(memory_space=pl.ANY)
    vmem = pl.BlockSpec(memory_space=pltpu.VMEM)
    dma = pltpu.SemaphoreType.DMA
    recon, toks, cots, acts, grads = pl.pallas_call(
        functools.partial(fused_kernel, cot_scale),
        out_shape=(
            jax.ShapeDtypeStruct((rows, width), BF16),
            jax.ShapeDtypeStruct((2, lat_count, rows, half), BF16),
            jax.ShapeDtypeStruct((2, lat_count, rows, half), BF16),
            jax.ShapeDtypeStruct((2, group_rows, latents), BF16),
            jax.ShapeDtypeStruct((2, group_rows, latents), BF16),
        ),
        in_specs=[hbm, hbm, vmem, hbm, vmem, pl.BlockSpec(memory_space=pltpu.SMEM)],
        out_specs=(vmem, hbm, hbm, hbm, hbm),
        scratch_shapes=[
            pltpu.VMEM((width, latents), BF16),
            pltpu.VMEM((latents, width), BF16),
            pltpu.VMEM((lat_count, rows, width), BF16),
            pltpu.VMEM((lat_count, rows, half), BF16),
            pltpu.VMEM((lat_count, rows, width), BF16),
            pltpu.VMEM((lat_count, rows, half), BF16),
            pltpu.VMEM((lat_count, rows, width), BF16),
            pltpu.VMEM((lat_count // NC, rows, width), BF16),
            pltpu.VMEM((NZ, rows, width), BF16),
            pltpu.VMEM((NZ, rows, width), BF16),
            pltpu.VMEM((NZ, rows, width), BF16),
            pltpu.VMEM((NZ, rows, width), BF16),
            pltpu.VMEM((group_rows, latents), F32),
            pltpu.VMEM((group_rows, latents), BF16),
            pltpu.VMEM((group_rows, latents), BF16),
            pltpu.VMEM((group_rows, latents), BF16),
            pltpu.VMEM((group_rows, latents), BF16),
            dma((11,)),
            dma((50,)), dma((32,)), dma((16,)),
            dma((50,)), dma((32,)), dma((16,)),
            dma((30,)), dma((16,)), dma((8,)), dma((8,)),
            dma((2,)), dma((2,)),
        ],
        compiler_params=pltpu.CompilerParams(
            collective_id=0, has_side_effects=True, vmem_limit_bytes=56 * 1024 * 1024
        ),
        name="fused_step",
    )(tokens, enc_weight, enc_bias[None, :], dec_weight, dec_bias[None, :], active_blocks)
    enc_grad = contract_rows(toks.reshape(2 * group_rows, half), grads.reshape(2 * group_rows, latents))
    dec_grad = contract_rows(acts.reshape(2 * group_rows, latents), cots.reshape(2 * group_rows, half))
    return recon, enc_grad, dec_grad


def shards(tokens, enc_weight, enc_bias, dec_weight, dec_bias, active_blocks):
    tok_dev = tokens.shape[0]
    lat_count = lax.axis_size("lat")
    tok_count = lax.axis_size("tok")
    group_rows = tok_dev * lat_count
    latent_width = enc_weight.shape[1]
    block_count = active_blocks.shape[0]
    block_rows = group_rows // block_count
    blocks_here = latent_width // LB
    owner_index = lax.axis_index("lat")
    cot_scale = 1.0 / math.sqrt(group_rows * tok_count)
    block_ids = owner_index * blocks_here + jnp.arange(blocks_here, dtype=jnp.int32)
    block_hits = jnp.any(active_blocks[:, :, None] == block_ids[None, None, :], axis=1).astype(
        jnp.float32
    )
    latent_gate = jnp.repeat(block_hits, LB, axis=1)[:, None, :]
    bias_row = enc_bias[None, None, :]
    gathered = lax.all_gather(tokens, "lat", axis=0, tiled=True)
    pre_act = (
        jnp.dot(gathered, enc_weight, preferred_element_type=jnp.float32).reshape(
            block_count, block_rows, latent_width
        )
        + bias_row
    )
    activations = (
        (jax.nn.silu(pre_act) * latent_gate).astype(jnp.bfloat16).reshape(group_rows, latent_width)
    )
    bias_dec = dec_bias[None, :]
    partial_sum = jnp.dot(activations, dec_weight, preferred_element_type=jnp.float32)
    decoded_all = lax.psum(partial_sum.astype(jnp.bfloat16), "lat").astype(jnp.float32) + bias_dec
    cot_all = ((decoded_all - gathered.astype(jnp.float32)) * cot_scale).astype(jnp.bfloat16)
    decoded = lax.dynamic_slice_in_dim(decoded_all, owner_index * tok_dev, tok_dev, 0)
    dec_local = contract_rows(activations, cot_all)
    latent_grad = lax.dot_general(
        cot_all, dec_weight, (((1,), (1,)), ((), ())), preferred_element_type=jnp.float32
    )
    sigma = jax.nn.sigmoid(pre_act)
    slope = sigma * (1.0 + pre_act * (1.0 - sigma))
    pre_grad = (
        (latent_grad.reshape(block_count, block_rows, latent_width) * slope * latent_gate)
        .astype(jnp.bfloat16)
        .reshape(group_rows, latent_width)
    )
    enc_local = contract_rows(gathered, pre_grad)
    enc_grad, dec_grad = (
        lax.psum_scatter(
            enc_local.astype(jnp.bfloat16), "tok", scatter_dimension=0, tiled=True
        ).astype(jnp.float32),
        lax.psum_scatter(
            dec_local.astype(jnp.bfloat16), "tok", scatter_dimension=1, tiled=True
        ).astype(jnp.float32),
    )
    return (decoded.astype(jnp.bfloat16), enc_grad, dec_grad)


def solution(mesh):
    placed = (
        P(("tok", "lat"), None),
        P(None, "lat"),
        P("lat"),
        P("lat", None),
        P(),
        P("tok", None),
    )
    fits = mesh.shape["tok"] == 2 and mesh.shape["lat"] == NZ * NX * NC
    return jax.shard_map(
        fused_shards if fits else shards,
        mesh=mesh,
        in_specs=placed,
        out_specs=(P(("tok", "lat"), None), P("tok", "lat"), P("lat", "tok")),
        check_vma=False,
    )
```
